32 devices in a mesh: seq: 16 (over z, x, core), grp: 2 (over y).
Axes of the slice: x: 2, y: 2, z: 4, core: 2. Of those that a mesh axis runs over, the one named last changes fastest.
Arguments:
- prefill_queries: bfloat16 [1024, 4096], P('seq', 'grp'), may hold values from -6 to 6
- prefill_keys: bfloat16 [1024, 512], P('seq', 'grp'), may hold values from -6 to 6
- prefill_values: bfloat16 [1024, 512], P('seq', 'grp'), may hold values from -6 to 6
- block_mask: int32 [16, 16], replicated, may hold values 0 or 1
- bit_widths: int32 [4], P('grp'), may hold values from 3 to 8
- scale_exps: int32 [4], P('grp'), may hold values from 1 to 4
- decode_queries: bfloat16 [4, 32, 4096], P(None, 'seq', 'grp'), may hold values from -6 to 6
- new_keys: bfloat16 [4, 32, 512], P(None, 'seq', 'grp'), may hold values from -6 to 6
- new_values: bfloat16 [4, 32, 512], P(None, 'seq', 'grp'), may hold values from -6 to 6
- context_len: int32 [32], P('seq'), may hold values from 1 to 1024
Outputs:
- prefill_out: bfloat16 [1024, 4096], P('seq', 'grp')
- decode_out: bfloat16 [4, 32, 4096], P(None, 'seq', 'grp')
The draws below stay inside these ranges and needn't reach their ends.
All inputs are finite; a program needn't handle non-finite values.
Results may differ from the reference program's by a relative error of at most 0.012.
Values may be sent and summed in bfloat16 or wider, within the bound.
No kernel may reach another device: no remote copies, remote signals or barrier semaphores. Data moves between devices by JAX's collectives and lax.ppermute only.
A program may use at most 64 MiB of HBM per device.

```python
import math
import jax
import jax.numpy as jnp
from jax import lax

HEADS = 32
KV_HEADS = 4
HEAD = 128
TOK_DEV = 64
ROW_DEV = 2
STEPS = 4
TOKENS = 1024
ROWS = 32
BLOCKS = 16


def prefill_pair(key):
    query_seed, key_seed = jax.random.split(key, 2)
    queries = jnp.clip(jax.random.normal(query_seed, (TOKENS, HEADS * HEAD), jnp.float32), -6.0, 6.0)
    keys_drawn = jnp.clip(jax.random.normal(key_seed, (TOKENS, KV_HEADS * HEAD), jnp.float32), -6.0, 6.0)
    return (queries, keys_drawn)


def decode_pair(key):
    query_seed, key_seed = jax.random.split(key, 2)
    queries = jnp.clip(jax.random.normal(query_seed, (STEPS, ROWS, HEADS * HEAD), jnp.float32), -6.0, 6.0)
    keys_drawn = jnp.clip(jax.random.normal(key_seed, (STEPS, ROWS, KV_HEADS * HEAD), jnp.float32), -6.0, 6.0)
    return (queries, keys_drawn)


def draw_prefill_queries(key, part):
    return prefill_pair(jax.random.fold_in(key, 11))[0].astype(jnp.bfloat16)


def draw_prefill_keys(key, part):
    return prefill_pair(jax.random.fold_in(key, 11))[1].astype(jnp.bfloat16)


def draw_decode_queries(key, part):
    return decode_pair(jax.random.fold_in(key, 23))[0].astype(jnp.bfloat16)


def draw_new_keys(key, part):
    return decode_pair(jax.random.fold_in(key, 23))[1].astype(jnp.bfloat16)


def place_ends(result, rng, smallest, largest):
    longest = result.shape.index(max(result.shape))
    spots = []
    for shift in (0, 1):
        where = [jax.random.randint(jax.random.fold_in(rng, axis), (), 0, length) for axis, length in enumerate(result.shape)]
        where[longest] = (where[longest] + shift) % result.shape[longest]
        spots.append(tuple(where))
    return result.at[spots[0]].set(smallest).at[spots[1]].set(largest)


def block_levels(rng, extent, cuts, smallest, top_value):
    loudness = 1.0
    for position, blocks in cuts:
        draws = jax.random.uniform(jax.random.fold_in(jax.random.fold_in(rng, 6), position), (blocks,), jnp.float32, smallest / len(cuts), top_value / len(cuts))
        loudness = loudness * jnp.repeat(jnp.exp(draws), extent[position] // blocks).reshape((-1,) + (1,) * (len(extent) - 1 - position))
    return loudness


def centred(own_key, shape, spread, limit, cuts=(), kind=jnp.bfloat16):
    values = jax.random.normal(own_key, shape, jnp.float32) * spread
    if len(cuts) > 0:
        values = block_levels(own_key, shape, cuts, -0.22, 0.18) * values
    return jnp.clip(values, min=-limit, max=limit).astype(kind)


def setup_inputs(seed: int = 0) -> dict:
    arg_keys = jax.random.split(jax.random.key(seed), 11)
    return {
        "prefill_queries": draw_prefill_queries(jax.random.fold_in(arg_keys[10], 71), 0),
        "prefill_keys": draw_prefill_keys(jax.random.fold_in(arg_keys[10], 71), 0),
        "prefill_values": centred(arg_keys[2], (TOKENS, KV_HEADS * HEAD), 1.0, 6.0, ((0, 16), (1, 2))),
        "block_mask": place_ends((jax.random.randint(arg_keys[3], (BLOCKS, BLOCKS), 0, 2) < 1).astype(jnp.int32), jax.random.fold_in(arg_keys[3], 1), 0, 1),
        "bit_widths": place_ends(jax.random.randint(arg_keys[4], (KV_HEADS,), 3, 9), jax.random.fold_in(arg_keys[4], 1), 3, 8).astype(jnp.int32),
        "scale_exps": place_ends(jax.random.randint(arg_keys[5], (KV_HEADS,), 1, 5), jax.random.fold_in(arg_keys[5], 1), 1, 4).astype(jnp.int32),
        "decode_queries": draw_decode_queries(jax.random.fold_in(arg_keys[10], 71), 0),
        "new_keys": draw_new_keys(jax.random.fold_in(arg_keys[10], 71), 0),
        "new_values": centred(arg_keys[8], (STEPS, ROWS, KV_HEADS * HEAD), 1.0, 6.0, ((1, 16), (2, 2))),
        "context_len": place_ends(jax.random.randint(arg_keys[9], (ROWS,), 1, TOKENS + 1), jax.random.fold_in(arg_keys[9], 1), 1, TOKENS).astype(jnp.int32),
    }


very_low = -1e+30
norm_eps = 1e-06

def sign_table(order):
    positions = jnp.arange(order, dtype=jnp.int32)
    common_bits = positions[:, None] & positions[None, :]
    parity = jnp.zeros((order, order), jnp.int32)
    for bit_number in range(order.bit_length() - 1):
        parity = parity + (common_bits >> bit_number & 1)
    return (1 - 2 * (parity % 2)).astype(jnp.float32)

def level_terms(bit_widths, scale_exps):
    clip_level = 2.0 ** (bit_widths.astype(jnp.float32) - 1.0) - 1.0
    forward = 2.0 ** scale_exps.astype(jnp.float32) / math.sqrt(HEAD)
    backward = 2.0 ** (-scale_exps.astype(jnp.float32)) / math.sqrt(HEAD)
    return (clip_level, forward, backward)

def encode_rows(shaped, sign_matrix, clip_level, forward):
    rotated = jnp.dot(shaped, sign_matrix, preferred_element_type=jnp.float32)
    levels = jnp.floor(rotated * forward[:, None] + 0.5)
    limited = jnp.clip(levels, -clip_level[:, None], clip_level[:, None])
    return limited.astype(jnp.bfloat16)

def decode_rows(encoded, sign_matrix, backward):
    restored = jnp.dot(encoded, sign_matrix, preferred_element_type=jnp.float32)
    return (restored * backward[:, None]).astype(jnp.bfloat16)

def rounded(weights):
    return lax.optimization_barrier(weights.astype(jnp.bfloat16)).astype(jnp.float32)

def head_norm(attn):
    mean_square = lax.optimization_barrier(jnp.sum(attn * attn, axis=-1, keepdims=True)) / (HEADS * HEAD)
    return (attn * lax.rsqrt(mean_square + norm_eps)).astype(jnp.bfloat16)

def reference(prefill_queries, prefill_keys, prefill_values, block_mask, bit_widths, scale_exps, decode_queries, new_keys, new_values, context_len):
    group_size = HEADS // KV_HEADS
    score_scale = 1.0 / math.sqrt(HEAD)
    sign_matrix = sign_table(HEAD).astype(jnp.bfloat16)
    clip_level, forward, backward = level_terms(bit_widths, scale_exps)
    key_rows = prefill_keys.reshape(TOKENS, KV_HEADS, HEAD)
    value_rows = prefill_values.reshape(TOKENS, KV_HEADS, HEAD)
    keys_wide = key_rows.astype(jnp.float32)
    values_wide = value_rows.astype(jnp.float32)
    key_pos = jnp.arange(TOKENS, dtype=jnp.int32)
    key_block = key_pos // TOK_DEV

    def prefill_block(block_index):
        queries = lax.dynamic_slice_in_dim(prefill_queries, block_index * TOK_DEV, TOK_DEV, 0)
        queries = queries.reshape(TOK_DEV, KV_HEADS, group_size, HEAD).astype(jnp.float32)
        query_pos = block_index * TOK_DEV + jnp.arange(TOK_DEV, dtype=jnp.int32)
        mask_row = block_mask[block_index]
        block_open = (key_block == block_index) | (mask_row[key_block] == 1)
        allowed = ((key_pos[None, :] <= query_pos[:, None]) & block_open[None, :])[:, None, None, :]
        scores = jnp.einsum('tkgd,skd->tkgs', queries, keys_wide) * score_scale
        masked = jnp.where(allowed, scores, very_low)
        top = lax.optimization_barrier(jnp.max(masked, axis=-1, keepdims=True))
        weights = jnp.where(allowed, jnp.exp(masked - top), 0.0)
        weight_sum = lax.optimization_barrier(jnp.sum(weights, axis=-1))
        mixed = jnp.einsum('tkgs,skd->tkgd', rounded(weights), values_wide)
        return (mixed / weight_sum[..., None]).reshape(TOK_DEV, HEADS * HEAD)
    prefill_attn = lax.map(prefill_block, jnp.arange(BLOCKS, dtype=jnp.int32)).reshape(TOKENS, HEADS * HEAD)
    cache_keys = decode_rows(encode_rows(key_rows, sign_matrix, clip_level, forward), sign_matrix, backward).astype(jnp.float32)
    cache_values = decode_rows(encode_rows(value_rows, sign_matrix, clip_level, forward), sign_matrix, backward).astype(jnp.float32)
    all_queries = decode_queries.reshape(STEPS, ROWS, KV_HEADS, group_size, HEAD).astype(jnp.float32)
    own_keys = new_keys.reshape(STEPS, ROWS, KV_HEADS, HEAD).astype(jnp.float32)
    own_values = new_values.reshape(STEPS, ROWS, KV_HEADS, HEAD).astype(jnp.float32)
    step_pos = jnp.arange(STEPS, dtype=jnp.int32)
    own_allowed = (step_pos[None, :] <= step_pos[:, None])[:, None, None, None, :]

    def decode_block(block_index):
        queries = lax.dynamic_slice_in_dim(all_queries, block_index * ROW_DEV, ROW_DEV, 1)
        block_keys = lax.dynamic_slice_in_dim(own_keys, block_index * ROW_DEV, ROW_DEV, 1)
        block_values = lax.dynamic_slice_in_dim(own_values, block_index * ROW_DEV, ROW_DEV, 1)
        limits = lax.dynamic_slice_in_dim(context_len, block_index * ROW_DEV, ROW_DEV, 0)
        cache_open = (key_pos[None, :] < limits[:, None])[None, :, None, None, :]
        cache_scores = jnp.einsum('trkgd,pkd->trkgp', queries, cache_keys) * score_scale
        own_scores = jnp.einsum('trkgd,urkd->trkgu', queries, block_keys) * score_scale
        cache_masked = jnp.where(cache_open, cache_scores, very_low)
        own_masked = jnp.where(own_allowed, own_scores, very_low)
        top = jnp.maximum(lax.optimization_barrier(jnp.max(cache_masked, axis=-1)), lax.optimization_barrier(jnp.max(own_masked, axis=-1)))[..., None]
        cache_weights = jnp.where(cache_open, jnp.exp(cache_masked - top), 0.0)
        own_weights = jnp.where(own_allowed, jnp.exp(own_masked - top), 0.0)
        weight_sum = lax.optimization_barrier(jnp.sum(cache_weights, axis=-1)) + lax.optimization_barrier(jnp.sum(own_weights, axis=-1))
        mixed = jnp.einsum('trkgp,pkd->trkgd', rounded(cache_weights), cache_values)
        mixed = mixed + jnp.einsum('trkgu,urkd->trkgd', rounded(own_weights), block_values)
        return (mixed / weight_sum[..., None]).reshape(STEPS, ROW_DEV, HEADS * HEAD)
    stacked = lax.map(decode_block, jnp.arange(BLOCKS, dtype=jnp.int32))
    decode_attn = jnp.moveaxis(stacked, 0, 1).reshape(STEPS, ROWS, HEADS * HEAD)
    return (head_norm(prefill_attn), head_norm(decode_attn))
```

```python
import functools
import math

import jax
import jax.numpy as jnp
import numpy as np
from jax import lax
from jax.experimental import pallas as pl
from jax.experimental.pallas import tpu as pltpu
from jax.sharding import PartitionSpec as P

HEADS = 32
KV_HEADS = 4
HEAD = 128
STEPS = 4
GROUP = HEADS // KV_HEADS
LANES = 128

very_low = -1e30
norm_eps = 1e-06
inv_root = np.float32(1.0) / np.float32(math.sqrt(HEAD))
exp_scale = np.float32(math.log2(math.e) / math.sqrt(HEAD))


def exchange_orders(size):
    bits = []
    bit = size // 2
    while bit >= 2:
        bits.append(bit)
        bit //= 2
    if len(bits) < 3:
        return bits, bits
    return [bits[0], bits[-1]] + bits[1:-1], [bits[1], bits[0]] + bits[2:]


def slot_offsets(order):
    offsets = [0]
    for mask in order:
        offsets = offsets + [offset ^ mask for offset in offsets]
    return offsets


def slot_blocks(size, seq_index):
    order_even, order_odd = exchange_orders(size)
    even, odd = slot_offsets(order_even), slot_offsets(order_odd)
    is_even = seq_index % 2 == 0
    own = [jnp.where(is_even, seq_index ^ a, seq_index ^ b) for a, b in zip(even, odd)]
    twin = [jnp.where(is_even, seq_index ^ 1 ^ b, seq_index ^ 1 ^ a) for a, b in zip(even, odd)]
    return own + twin


def gather_steps(array, size):
    order_even, order_odd = exchange_orders(size)
    for mask_even, mask_odd in zip(order_even, order_odd):
        pairs = [(i, i ^ (mask_odd if i % 2 else mask_even)) for i in range(size)]
        array = jnp.concatenate([array, lax.ppermute(array, "seq", pairs)], axis=0)
    twin = lax.ppermute(array, "seq", [(i, i ^ 1) for i in range(size)])
    return array, twin


def hadamard():
    index = np.arange(HEAD)
    common = index[:, None] & index[None, :]
    parity = np.zeros((HEAD, HEAD), np.int32)
    for bit in range(HEAD.bit_length() - 1):
        parity += (common >> bit) & 1
    return (1 - 2 * (parity % 2)).astype(np.float32)


def sign_rows():
    row = lax.broadcasted_iota(jnp.int32, (HEAD, HEAD), 0)
    col = lax.broadcasted_iota(jnp.int32, (HEAD, HEAD), 1)
    common = row & col
    for shift in (4, 2, 1):
        common = common ^ (common >> shift)
    return (1 - 2 * (common & 1)).astype(jnp.float32).astype(jnp.bfloat16)


def recode(rows, signs, level, forward, backward):
    rotated = jnp.dot(rows, signs, preferred_element_type=jnp.float32)
    codes = jnp.clip(jnp.floor(rotated * forward + 0.5), -level, level).astype(jnp.bfloat16)
    restored = jnp.dot(codes, signs, preferred_element_type=jnp.float32)
    return (restored * backward).astype(jnp.bfloat16)


def code_terms(widths_ref, exps_ref, head):
    level = ((1 << (widths_ref[head] - 1)) - 1).astype(jnp.float32)
    scale = (1 << exps_ref[head]).astype(jnp.float32)
    return level, scale * inv_root, inv_root / scale


def nt(a, b):
    return lax.dot_general(a, b, (((1,), (1,)), ((), ())), preferred_element_type=jnp.float32)


def per_lane(pair, lane, token_block):
    return jnp.where(lane < token_block, pair[0], pair[1])


def score_kernel(size, info_ref, mask_ref, widths_ref, exps_ref, ctx_ref, q_ref, dq_ref, own_ref,
                 twin_ref, nk_ref, p_ref, l_ref, dp_ref, dl_ref, s_ref, restored_ref, ds_ref):
    tokens = q_ref.shape[0]
    kv_local = widths_ref.shape[0]
    row_count = ctx_ref.shape[0]
    half = own_ref.shape[0]
    keys = 2 * half
    chunk = min(256, half)
    seq_index = info_ref[0]
    blocks = slot_blocks(size, seq_index)
    lane = lax.broadcasted_iota(jnp.int32, (1, LANES), 1)
    slots = LANES // tokens
    opens = [
        jnp.where((b < seq_index) & (mask_ref[seq_index, b] == 1), 0.0, very_low) for b in blocks
    ]
    opens[0] = jnp.float32(0.0)
    bias = jnp.concatenate(
        [
            per_lane(opens[slots * i : slots * i + slots], lane, tokens)
            for i in range(keys // LANES)
        ],
        axis=1,
    )
    position = jnp.concatenate(
        [
            per_lane(
                [blocks[slots * i] * tokens, (blocks[slots * i + 1] - 1) * tokens], lane, tokens
            )
            + lane
            for i in range(keys // LANES)
        ],
        axis=1,
    )
    signs = sign_rows()
    rows = GROUP * tokens
    step_rows = min(32, tokens)
    for head in range(kv_local):
        lanes = pl.ds(head * HEAD, HEAD)
        q = jnp.concatenate(
            [q_ref[:, pl.ds((head * GROUP + g) * HEAD, HEAD)] for g in range(GROUP)], axis=0
        )
        level, forward, backward = code_terms(widths_ref, exps_ref, head)
        for start in range(0, keys, chunk):
            source = own_ref if start < half else twin_ref
            k = source[pl.ds(start % half, chunk), lanes]
            s_ref[:, pl.ds(start, chunk)] = nt(q, k)
            restored_ref[pl.ds(start, chunk), :] = recode(k, signs, level, forward, backward)
        restored_ref[pl.ds(keys, LANES), :] = jnp.zeros((LANES, HEAD), jnp.bfloat16)
        restored_ref[pl.ds(keys, nk_ref.shape[0]), :] = nk_ref[:, lanes]

        for start in range(0, rows, step_rows):
            first = start % tokens
            scores = s_ref[pl.ds(start, step_rows), :] + bias
            row = lax.broadcasted_iota(jnp.int32, (step_rows, LANES), 0) + first
            col = lax.broadcasted_iota(jnp.int32, (step_rows, LANES), 1)
            corner = jnp.where((col < tokens) & (col > row), very_low, scores[:, :LANES])
            scores = jnp.concatenate([corner, scores[:, LANES:]], axis=1)
            top = jnp.max(scores, axis=1, keepdims=True)
            weights = jnp.exp2((scores - top) * exp_scale)
            l_ref[pl.ds(head * rows + start, step_rows), :] = jnp.sum(weights, axis=1, keepdims=True)
            p_ref[pl.ds(head * rows + start, step_rows), :] = weights.astype(jnp.bfloat16)

        dq_rows = dq_ref.shape[0]
        dq = jnp.concatenate(
            [
                dq_ref[:, pl.ds((head * GROUP + g) * HEAD, HEAD)].astype(jnp.float32)
                for g in range(GROUP)
            ],
            axis=0,
        ).astype(jnp.bfloat16)
        d_rows = GROUP * dq_rows
        scores = nt(dq, restored_ref[...])
        row = lax.broadcasted_iota(jnp.int32, (d_rows, 1), 0) % dq_rows
        row_id, step = row % row_count, row // row_count
        limit = jnp.zeros((d_rows, 1), jnp.int32)
        for r in range(row_count):
            limit = jnp.where(row_id == r, ctx_ref[r], limit)
        cached = jnp.where(position < limit, scores[:, :keys], very_low)
        new_ok = (lane < dq_rows) & (lane % row_count == row_id) & (lane // row_count <= step)
        fresh = jnp.where(new_ok, scores[:, keys:], very_low)
        scores = jnp.concatenate([cached, fresh], axis=1)
        top = jnp.max(scores, axis=1, keepdims=True)
        weights = jnp.exp2((scores - top) * exp_scale)
        dl_ref[pl.ds(head * d_rows, d_rows), :] = jnp.sum(weights, axis=1, keepdims=True)
        dp_ref[pl.ds(head * d_rows, d_rows), :] = weights.astype(jnp.bfloat16)


def value_kernel(widths_ref, exps_ref, p_ref, l_ref, dp_ref, dl_ref, own_ref, twin_ref, nv_ref,
                 out_ref, dout_ref, sq_ref, restored_ref):
    kv_local = widths_ref.shape[0]
    half = own_ref.shape[0]
    keys = 2 * half
    chunk = min(256, half)
    rows = p_ref.shape[0] // kv_local
    d_rows = dp_ref.shape[0] // kv_local
    tokens = rows // GROUP
    dq_rows = d_rows // GROUP
    signs = sign_rows()
    squares = jnp.zeros((tokens, HEAD), jnp.float32)
    d_squares = jnp.zeros((dq_rows, HEAD), jnp.float32)
    for head in range(kv_local):
        lanes = pl.ds(head * HEAD, HEAD)
        level, forward, backward = code_terms(widths_ref, exps_ref, head)
        head_rows = pl.ds(head * rows, rows)
        total = jnp.dot(
            p_ref[head_rows, pl.ds(0, half)], own_ref[:, lanes], preferred_element_type=jnp.float32
        ) + jnp.dot(
            p_ref[head_rows, pl.ds(half, half)], twin_ref[:, lanes],
            preferred_element_type=jnp.float32,
        )
        total = total / l_ref[head_rows, :]
        for g in range(GROUP):
            piece = total[g * tokens : (g + 1) * tokens]
            out_ref[:, pl.ds((head * GROUP + g) * HEAD, HEAD)] = piece
            squares = squares + piece * piece
        for start in range(0, keys, chunk):
            source = own_ref if start < half else twin_ref
            v = source[pl.ds(start % half, chunk), lanes]
            restored_ref[pl.ds(start, chunk), :] = recode(v, signs, level, forward, backward)
        restored_ref[pl.ds(keys, LANES), :] = jnp.zeros((LANES, HEAD), jnp.bfloat16)
        restored_ref[pl.ds(keys, nv_ref.shape[0]), :] = nv_ref[:, lanes]
        d_head_rows = pl.ds(head * d_rows, d_rows)
        d_total = jnp.dot(
            dp_ref[d_head_rows, :], restored_ref[...], preferred_element_type=jnp.float32
        )
        d_total = d_total / dl_ref[d_head_rows, :]
        for g in range(GROUP):
            piece = d_total[g * dq_rows : (g + 1) * dq_rows]
            dout_ref[:, pl.ds((head * GROUP + g) * HEAD, HEAD)] = piece
            d_squares = d_squares + piece * piece
    sq_ref[pl.ds(0, tokens), :] = jnp.broadcast_to(
        jnp.sum(squares, axis=1, keepdims=True), (tokens, HEAD)
    )
    sq_ref[pl.ds(tokens, dq_rows), :] = jnp.broadcast_to(
        jnp.sum(d_squares, axis=1, keepdims=True), (dq_rows, HEAD)
    )


def scale_kernel(attn_ref, dattn_ref, mine_ref, theirs_ref, out_ref, dout_ref):
    tokens, width = attn_ref.shape
    steps, row_count, _ = dout_ref.shape
    factor = lax.rsqrt((mine_ref[...] + theirs_ref[...]) / (HEADS * HEAD) + norm_eps)
    for start in range(0, width, HEAD):
        lanes = pl.ds(start, HEAD)
        out_ref[:, lanes] = (attn_ref[:, lanes] * factor[:tokens]).astype(jnp.bfloat16)
        piece = (dattn_ref[:, lanes] * factor[tokens:]).astype(jnp.bfloat16)
        for step in range(steps):
            dout_ref[step, :, lanes] = piece[step * row_count : (step + 1) * row_count]


def local(size, prefill_queries, prefill_keys, prefill_values, block_mask, bit_widths, scale_exps,
          decode_queries, new_keys, new_values, context_len):
    tokens, width = prefill_queries.shape
    kv_local = bit_widths.shape[0]
    row_count = context_len.shape[0]
    dq_rows = STEPS * row_count
    keys = tokens * size
    rows = kv_local * GROUP * tokens
    d_rows = kv_local * GROUP * dq_rows
    seq_index = lax.axis_index("seq").astype(jnp.int32).reshape(1)
    dq = decode_queries.reshape(dq_rows, width)
    nk = new_keys.reshape(dq_rows, kv_local * HEAD)
    nv = new_values.reshape(dq_rows, kv_local * HEAD)
    smem = pl.BlockSpec(memory_space=pltpu.SMEM)
    vmem = pl.BlockSpec(memory_space=pltpu.VMEM)
    shape = jax.ShapeDtypeStruct
    limit = 20 * 2**20 if keys <= 2048 else 60 * 2**20

    own_k, twin_k = gather_steps(prefill_keys, size)
    own_v, twin_v = gather_steps(prefill_values, size)

    weights = pl.pallas_call(
        functools.partial(score_kernel, size),
        out_shape=(
            shape((rows, keys), jnp.bfloat16),
            shape((rows, 1), jnp.float32),
            shape((d_rows, keys + LANES), jnp.bfloat16),
            shape((d_rows, 1), jnp.float32),
        ),
        in_specs=[smem] * 5 + [vmem] * 5,
        out_specs=(vmem,) * 4,
        scratch_shapes=[
            pltpu.VMEM((rows // kv_local, keys), jnp.float32),
            pltpu.VMEM((keys + LANES, HEAD), jnp.bfloat16),
            pltpu.VMEM((d_rows // kv_local, keys + LANES), jnp.float32),
        ],
        compiler_params=pltpu.CompilerParams(vmem_limit_bytes=limit),
        cost_estimate=pl.CostEstimate(
            flops=2 * rows * keys * HEAD, bytes_accessed=2 * rows * keys, transcendentals=rows * keys
        ),
        name="scores",
    )(seq_index, block_mask, bit_widths, scale_exps, context_len, prefill_queries, dq, own_k,
      twin_k, nk)

    attn, dattn, squares = pl.pallas_call(
        value_kernel,
        out_shape=(
            shape((tokens, width), jnp.float32),
            shape((dq_rows, width), jnp.float32),
            shape((tokens + dq_rows, HEAD), jnp.float32),
        ),
        in_specs=[smem] * 2 + [vmem] * 7,
        out_specs=(vmem,) * 3,
        scratch_shapes=[pltpu.VMEM((keys + LANES, HEAD), jnp.bfloat16)],
        compiler_params=pltpu.CompilerParams(vmem_limit_bytes=limit),
        cost_estimate=pl.CostEstimate(
            flops=2 * rows * keys * HEAD, bytes_accessed=2 * rows * keys, transcendentals=0
        ),
        name="values",
    )(bit_widths, scale_exps, *weights, own_v, twin_v, nv)

    theirs = lax.ppermute(squares, "grp", [(0, 1), (1, 0)])
    return pl.pallas_call(
        scale_kernel,
        out_shape=(
            shape((tokens, width), jnp.bfloat16),
            shape((STEPS, row_count, width), jnp.bfloat16),
        ),
        in_specs=[vmem] * 4,
        out_specs=(vmem,) * 2,
        compiler_params=pltpu.CompilerParams(vmem_limit_bytes=limit),
        name="scale",
    )(attn, dattn, squares, theirs)


def solution(mesh):
    placed = (
        P("seq", "grp"),
        P("seq", "grp"),
        P("seq", "grp"),
        P(),
        P("grp"),
        P("grp"),
        P(None, "seq", "grp"),
        P(None, "seq", "grp"),
        P(None, "seq", "grp"),
        P("seq"),
    )
    return jax.shard_map(
        functools.partial(local, mesh.shape["seq"]),
        mesh=mesh,
        in_specs=placed,
        out_specs=(P("seq", "grp"), P(None, "seq", "grp")),
        check_vma=False,
    )
```
